256 devices in a mesh: dp: 32 (over y, z), head: 8 (over x, core).
Axes of the slice: x: 4, y: 4, z: 8, core: 2. Of those that a mesh axis runs over, the one named last changes fastest.
Arguments:
- queries: bfloat16 [32768, 4096], P('dp', 'head'), may hold values from -6 to 6
- keys: bfloat16 [32768, 4096], P('dp', 'head'), may hold values from -6 to 6
- values: bfloat16 [32768, 4096], P('dp', 'head'), may hold values from -100 to 100
- out_grad: bfloat16 [32768, 4096], P('dp', 'head'), may hold values from -6 to 6
- norm_gain: float32 [4096], P('head'), may hold values from 0.1 to 1.9
- decay_table: float32 [16, 8], P('head'), may hold values from 0 to 0.52, as said below
- decay_index: int32 [16, 32768], P('head', 'dp'), may hold values from 0 to 7
- rollout_lengths: int32 [6], replicated, may hold values from 1 to 16384, 32768 in all
- move_partner: int32 [32], replicated, may hold values from 0 to 31, as said below
- move_slot: int32 [32], replicated, may hold values from 0 to 31, as said below
Outputs:
- query_grad: bfloat16 [32768, 4096], P('dp', 'head')
- key_grad: bfloat16 [32768, 4096], P('dp', 'head')
- value_grad: bfloat16 [32768, 4096], P('dp', 'head')
The draws below stay inside these ranges and needn't reach their ends.
Inputs may be any that keep to these rules, and one draw needn't show every extreme that they name: `decay_table`: positive rates. `rollout_lengths`: they sum to 32768. move_partner[d] is either d itself or a row whose index differs from d in exactly one bit, and the partner of the partner is the row itself. `move_slot`: one block of each row.
All inputs are finite; a program needn't handle non-finite values.
Results may differ from the reference program's by a relative error of at most 0.0063.
Values may be sent and summed in bfloat16 or wider, within the bound.
No kernel may reach another device: no remote copies, remote signals or barrier semaphores. Data moves between devices by JAX's collectives and lax.ppermute only.
A program may use at most 128 MiB of HBM per device.

```python
import math
import jax
import jax.numpy as jnp
import numpy as np
from jax import lax

HEAD_DIM = 256
RETENTION_HEADS = 16
DECAY_LEVELS = 8
BLOCK_LEN = 32
ROW_BLOCKS = 32
ROLLOUTS = 6
ROW_TOKENS = 1024
DATA_ROWS = 32
TOKEN_TOTAL = 32768
FEATURES = 4096


def draw_values(key, part):
    first_key = jax.random.fold_in(key, 0)
    head_of = (jnp.arange(FEATURES) // HEAD_DIM).astype(jnp.float32)
    column_scale = 10.0 ** (head_of / (RETENTION_HEADS - 1))
    base = jnp.clip(jax.random.normal(first_key, (TOKEN_TOTAL, FEATURES), jnp.float32), -6.0, 6.0)
    return (base * column_scale[None, :]).astype(jnp.bfloat16)


def draw_decay_table(key, part):
    permute_random_key, gradual_random_key, quick_random_key, spike_random_key = jax.random.split(key, 4)
    order = jax.random.permutation(permute_random_key, RETENTION_HEADS)
    fast_count = RETENTION_HEADS // 2
    is_fast = order < fast_count
    slow_base = jax.random.uniform(gradual_random_key, (RETENTION_HEADS,), jnp.float32, 0.1, 0.5) * math.log(10.0) / TOKEN_TOTAL
    fast_base = 1.0 / jax.random.uniform(quick_random_key, (RETENTION_HEADS,), jnp.float32, 30.0, 50.0)
    base_rate = jnp.where(is_fast, fast_base, slow_base)
    factors = jnp.array([0.5, 0.8, 1.25, 2.0], jnp.float32)
    steady_level = base_rate[:, None] * factors[None, :]
    loss_values = jax.random.uniform(spike_random_key, (RETENTION_HEADS, DECAY_LEVELS - 4), jnp.float32, 0.2, 0.4)
    spike_flags = -jnp.log(1.0 - loss_values)
    return jnp.concatenate([steady_level, spike_flags], axis=1).astype(jnp.float32)


def draw_decay_index(key, part):
    block_random_key, spike_random_key, level_random_key = jax.random.split(key, 3)
    spans = (TOKEN_TOTAL + 255) // 256
    steady_level = jax.random.randint(block_random_key, (RETENTION_HEADS, spans), 0, 4)
    steady_level = jnp.repeat(steady_level, 256, axis=1)[:, :TOKEN_TOTAL]
    is_spiking = jax.random.randint(spike_random_key, (RETENTION_HEADS, TOKEN_TOTAL), 0, 8192) == 0
    spike_level = jax.random.randint(level_random_key, (RETENTION_HEADS, TOKEN_TOTAL), 4, DECAY_LEVELS)
    return jnp.where(is_spiking, spike_level, steady_level).astype(jnp.int32)


def draw_move_partner(key, part):
    levels = DATA_ROWS.bit_length() - 1
    level_keys = jax.random.split(key, levels + 1)
    row_ids = jnp.arange(DATA_ROWS, dtype=jnp.int32)
    partner = row_ids
    for level in reversed(range(levels)):
        other = jnp.bitwise_xor(row_ids, 1 << level).astype(jnp.int32)
        flags = jax.random.randint(level_keys[level], (DATA_ROWS,), 0, 2)
        lower = jnp.minimum(row_ids, other)
        wanted = flags[lower] == 1
        unpaired = (partner == row_ids) & (partner[other] == other)
        partner = jnp.where(wanted & unpaired, other, partner).astype(jnp.int32)
    chosen = (jax.random.randint(level_keys[levels], (), 0, DATA_ROWS // 2) * 2).astype(jnp.int32)
    first_old = partner[chosen]
    second_old = partner[chosen + 1]
    partner = partner.at[first_old].set(first_old).at[second_old].set(second_old)
    partner = partner.at[chosen].set(chosen + 1).at[chosen + 1].set(chosen)
    return partner.astype(jnp.int32)


def draw_move_slot(key, part):
    slot_key, pick_key = jax.random.split(key, 2)
    slots = jax.random.randint(slot_key, (DATA_ROWS,), 0, ROW_BLOCKS)
    chosen = jax.random.randint(pick_key, (), 0, DATA_ROWS)
    return jnp.where(jnp.arange(DATA_ROWS) == chosen, ROW_BLOCKS - 1, slots).astype(jnp.int32)


def block_scale(rng, shape, cuts, low, high):
    def one(dim, blocks):
        steps = jax.random.uniform(jax.random.fold_in(jax.random.fold_in(rng, 6), dim), (blocks,), jnp.float32, low / len(cuts), high / len(cuts))
        return jnp.repeat(jnp.exp(steps), shape[dim] // blocks).reshape((-1,) + (1,) * (len(shape) - dim - 1))

    factor_of = one(*cuts[0])
    for cut in cuts[1:]:
        factor_of = factor_of * one(*cut)
    return factor_of


def split_up(count, total, most, skew):
    portions = [(1 << 20) // math.isqrt(standing ** skew) + 1 for standing in range(2, count + 1)]
    rest, holding = total - most - (count - 1), [1] * (count - 1)
    while rest > 0:
        free = [i for i in range(count - 1) if holding[i] < most]
        pool, left = sum([portions[i] for i in free]), rest
        for i in free:
            addition = min(most - holding[i], max(1, left * portions[i] // pool), rest)
            holding[i] = holding[i] + addition
            rest = rest - addition
    return np.array([most] + holding)


def uneven(rng, number_of, total, most, lean):
    if number_of == 2:
        one = jax.random.randint(rng, (), max(1, total - most), min(most, total - 1) + 1)
        return jnp.stack([one, total - one])
    tallies = jnp.asarray(split_up(number_of, total, most, lean), jnp.int32)
    couples = (number_of - 1) // 2
    giver, taker = tallies[1:1 + 2 * couples:2], tallies[2:2 + 2 * couples:2]
    margin = jnp.minimum(giver - 1, most - taker)
    passed = jax.random.randint(jax.random.fold_in(rng, 1), (couples,), 0, 1 << 20) % (margin + 1)
    tallies = tallies.at[1:1 + 2 * couples:2].set(giver - passed).at[2:2 + 2 * couples:2].set(taker + passed)
    return tallies[jax.random.permutation(jax.random.fold_in(rng, 2), number_of)]


def gaussian(stream_key, extent, spread, reach, pieces=(), kind=jnp.bfloat16):
    result = jax.random.normal(stream_key, extent, jnp.float32) * spread
    if len(pieces) > 0:
        result = block_scale(stream_key, extent, pieces, -0.22, 0.18) * result
    return jnp.clip(result, min=-reach, max=reach).astype(kind)


def setup_inputs(seed: int = 0) -> dict:
    key_of = jax.random.split(jax.random.key(seed), 11)
    queries = gaussian(key_of[0], (TOKEN_TOTAL, FEATURES), 1.0, 6.0, ((0, 32), (1, 8)))
    keys = gaussian(key_of[1], (TOKEN_TOTAL, FEATURES), 1.0, 6.0, ((0, 32), (1, 8)))
    values = draw_values(jax.random.fold_in(key_of[10], 71), 0)
    out_grad = gaussian(key_of[3], (TOKEN_TOTAL, FEATURES), 1.0, 6.0, ((0, 32), (1, 8)))
    norm_gain = jnp.clip(1.0 + 0.18 * jax.random.normal(key_of[4], (FEATURES,), jnp.float32), 0.1, 1.9)
    decay_table = draw_decay_table(jax.random.fold_in(key_of[10], 71), 0)
    decay_index = draw_decay_index(jax.random.fold_in(key_of[10], 71), 0)
    rollout_lengths = uneven(key_of[7], ROLLOUTS, TOKEN_TOTAL, TOKEN_TOTAL // 2, 2).astype(jnp.int32)
    move_partner = draw_move_partner(jax.random.fold_in(key_of[10], 71), 0)
    move_slot = draw_move_slot(jax.random.fold_in(key_of[10], 71), 0)
    return dict(queries=queries, keys=keys, values=values, out_grad=out_grad, norm_gain=norm_gain, decay_table=decay_table, decay_index=decay_index, rollout_lengths=rollout_lengths, move_partner=move_partner, move_slot=move_slot)


EPSILON = 1e-05
HIGHEST = lax.Precision.HIGHEST

def edge_factors(rate, flag):
    segment = jnp.cumsum(flag.astype(jnp.int32)).astype(jnp.int32)
    total = jnp.cumsum(rate, axis=1)
    first = jnp.where(segment[None, :] == 0, jnp.exp(-total), 0.0)
    last = jnp.where(segment[None, :] == segment[-1], jnp.exp(total - total[:, -1:]), 0.0)
    whole = jnp.where(segment[-1] == 0, jnp.exp(-total[:, -1]), 0.0)
    return (total, segment, first, last, whole)

def decay_matrix(total_row, segment):
    count = segment.shape[0]
    places = jnp.arange(count)
    inside = (segment[:, None] == segment[None, :]) & (places[:, None] >= places[None, :])
    return jnp.where(inside, jnp.exp(jnp.minimum(total_row[None, :] - total_row[:, None], 0.0)), 0.0)

def trade_blocks(stored, move_partner, move_slot):
    row_ids = jnp.arange(DATA_ROWS, dtype=jnp.int32)[:, None]
    block_ids = jnp.arange(ROW_BLOCKS, dtype=jnp.int32)[None, :]
    moved = block_ids == move_slot[:, None]
    source_row = jnp.where(moved, move_partner[:, None], row_ids).astype(jnp.int32)
    source_block = jnp.where(moved, move_slot[move_partner][:, None], block_ids).astype(jnp.int32)
    return stored[source_row, source_block]

def carry_step(state, item):
    local_row, whole = item
    return (whole[:, None, None] * state + local_row, state)

def round_half(array):
    return lax.optimization_barrier(array.astype(jnp.bfloat16)).astype(jnp.float32)

def reference(queries, keys, values, out_grad, norm_gain, decay_table, decay_index, rollout_lengths, move_partner, move_slot):

    def packed(array):
        shaped = array.reshape(DATA_ROWS, ROW_BLOCKS, BLOCK_LEN, FEATURES)
        return trade_blocks(shaped, move_partner, move_slot).reshape(DATA_ROWS, ROW_TOKENS, RETENTION_HEADS, HEAD_DIM)
    query_rows = packed(queries)
    key_rows = packed(keys)
    value_rows = packed(values)
    cotangent_rows = packed(out_grad).reshape(DATA_ROWS, ROW_TOKENS, FEATURES)
    index_stored = decay_index.T.reshape(DATA_ROWS, ROW_BLOCKS, BLOCK_LEN, RETENTION_HEADS)
    index_rows = trade_blocks(index_stored, move_partner, move_slot).reshape(DATA_ROWS, ROW_TOKENS, RETENTION_HEADS)
    level_ids = jnp.arange(DECAY_LEVELS, dtype=jnp.int32)
    rate_rows = lax.optimization_barrier(jnp.sum(jnp.where(index_rows[..., None] == level_ids, decay_table[None, None], 0.0), axis=-1))
    rate_rows = jnp.transpose(rate_rows, (0, 2, 1))
    starts = (jnp.cumsum(rollout_lengths) - rollout_lengths).astype(jnp.int32)
    position = jnp.arange(TOKEN_TOTAL, dtype=jnp.int32).reshape(DATA_ROWS, ROW_TOKENS)
    flag_rows = jnp.any(position[..., None] == starts, axis=-1)

    def local_state(inputs):
        key_row, value_row, rate, flag = inputs
        total, segment, first, last, whole = edge_factors(rate, flag)
        scaled = round_half(value_row.astype(jnp.float32) * last.T[:, :, None])
        state = jnp.einsum('shi,shj->hij', key_row.astype(jnp.float32), scaled, precision=HIGHEST)
        return (state, whole)
    local_states, wholes = lax.map(local_state, (key_rows, value_rows, rate_rows, flag_rows))
    zero_state = jnp.zeros((RETENTION_HEADS, HEAD_DIM, HEAD_DIM), jnp.float32)
    _, carry_in = lax.scan(carry_step, zero_state, (local_states, wholes))
    carry_in = round_half(carry_in)

    def forward_row(inputs):
        query_row, key_row, value_row, cotangent, rate, flag, state_in = inputs
        total, segment, first, last, whole = edge_factors(rate, flag)
        decay = jax.vmap(decay_matrix, (0, None))(total, segment)
        query_f = query_row.astype(jnp.float32)
        scores = jnp.einsum('thi,shi->hts', query_f, key_row.astype(jnp.float32), precision=HIGHEST)
        weights = (scores * decay / HEAD_DIM).astype(jnp.bfloat16)
        inner_part = jnp.einsum('hts,shj->thj', weights.astype(jnp.float32), value_row.astype(jnp.float32), precision=HIGHEST)
        cross_part = first.T[:, :, None] * jnp.einsum('thi,hij->thj', query_f, state_in, precision=HIGHEST) / HEAD_DIM
        retained = (inner_part + cross_part).reshape(ROW_TOKENS, FEATURES)
        scaled = norm_gain * cotangent.astype(jnp.float32)
        squares = lax.optimization_barrier(jnp.sum(retained * retained, axis=1))
        inner = lax.optimization_barrier(jnp.sum(scaled * retained, axis=1))
        recip = lax.rsqrt(squares / FEATURES + EPSILON)
        norm_grad = (recip[:, None] * scaled - (recip ** 3 * inner / FEATURES)[:, None] * retained).astype(jnp.bfloat16)
        grad_heads = norm_grad.reshape(ROW_TOKENS, RETENTION_HEADS, HEAD_DIM)
        weighted = round_half(grad_heads.astype(jnp.float32) * first.T[:, :, None])
        back_local = jnp.einsum('thi,thj->hij', query_f, weighted, precision=HIGHEST) / HEAD_DIM
        return (grad_heads, back_local)
    grad_rows, back_locals = lax.map(forward_row, (query_rows, key_rows, value_rows, cotangent_rows, rate_rows, flag_rows, carry_in))
    _, carry_back = lax.scan(carry_step, zero_state, (back_locals, wholes), reverse=True)
    carry_back = round_half(carry_back)

    def backward_row(inputs):
        query_row, key_row, value_row, grad_heads, rate, flag, state_in, state_back = inputs
        total, segment, first, last, whole = edge_factors(rate, flag)
        decay = jax.vmap(decay_matrix, (0, None))(total, segment)
        query_f = query_row.astype(jnp.float32)
        key_f = key_row.astype(jnp.float32)
        value_f = value_row.astype(jnp.float32)
        grad_f = grad_heads.astype(jnp.float32)
        scores = jnp.einsum('thi,shi->hts', query_f, key_f, precision=HIGHEST)
        weights = round_half(scores * decay / HEAD_DIM)
        grad_scores = jnp.einsum('thj,shj->hts', grad_f, value_f, precision=HIGHEST)
        grad_weights = round_half(grad_scores * decay / HEAD_DIM)
        query_part = jnp.einsum('hts,shi->thi', grad_weights, key_f, precision=HIGHEST)
        query_part = query_part + first.T[:, :, None] * jnp.einsum('thj,hij->thi', grad_f, state_in, precision=HIGHEST) / HEAD_DIM
        key_part = jnp.einsum('hts,thi->shi', grad_weights, query_f, precision=HIGHEST)
        key_part = key_part + last.T[:, :, None] * jnp.einsum('shj,hij->shi', value_f, state_back, precision=HIGHEST)
        value_part = jnp.einsum('hts,thj->shj', weights, grad_f, precision=HIGHEST)
        value_part = value_part + last.T[:, :, None] * jnp.einsum('shi,hij->shj', key_f, state_back, precision=HIGHEST)
        return (query_part.reshape(ROW_TOKENS, FEATURES).astype(jnp.bfloat16), key_part.reshape(ROW_TOKENS, FEATURES).astype(jnp.bfloat16), value_part.reshape(ROW_TOKENS, FEATURES).astype(jnp.bfloat16))
    query_back, key_back, value_back = lax.map(backward_row, (query_rows, key_rows, value_rows, grad_rows, rate_rows, flag_rows, carry_in, carry_back))

    def stored(array):
        shaped = array.reshape(DATA_ROWS, ROW_BLOCKS, BLOCK_LEN, FEATURES)
        return trade_blocks(shaped, move_partner, move_slot).reshape(TOKEN_TOTAL, FEATURES)
    return (stored(query_back), stored(key_back), stored(value_back))
```

```python
import jax
import jax.numpy as jnp
from jax import lax
from jax.experimental import pallas as pl
from jax.experimental.pallas import tpu as pltpu
from jax.sharding import PartitionSpec as P

HEAD_DIM = 256
BLOCK_LEN = 32
FEATURES = 4096


EPSILON = 1e-05


ROWS = 32
ROW_BITS = 5
SLAB = 16
EXTRA = 8


def swap_with(buffer, apart):
    found = buffer
    for bit in range(ROW_BITS):
        pairs = [(d, d ^ (1 << bit)) for d in range(ROWS)]
        came = lax.ppermute(buffer, "dp", pairs)
        found = jnp.where(apart == (1 << bit), came, found)
    return found


def carry_body(reverse, got_ref, out_ref):
    state = jnp.zeros((SLAB, HEAD_DIM), jnp.float32)
    for turn in range(ROWS):
        d = ROWS - 1 - turn if reverse else turn
        out_ref[d] = state.astype(jnp.bfloat16)
        got = got_ref[d].astype(jnp.float32)
        decay = got[SLAB : SLAB + 1] + got[SLAB + 1 : SLAB + 2] + got[SLAB + 2 : SLAB + 3]
        state = decay * state + got[:SLAB]


def entering(states, whole, reverse):
    slabs = states.astype(jnp.bfloat16).reshape(ROWS, SLAB, HEAD_DIM)
    high = lax.reduce_precision(whole, 8, 7)
    middle = lax.reduce_precision(whole - high, 8, 7)
    low = whole - high - middle
    thirds = jnp.stack([high, middle, low], axis=1).astype(jnp.bfloat16)
    extra = jnp.pad(thirds, ((0, 0), (0, EXTRA - 3)))
    extra = jnp.repeat(extra, ROWS // whole.shape[0], axis=0)
    extra = jnp.broadcast_to(extra[:, :, None], (ROWS, EXTRA, HEAD_DIM))
    got = lax.all_to_all(jnp.concatenate([slabs, extra], axis=1), "dp", 0, 0, tiled=True)
    out = pl.pallas_call(
        lambda g, o: carry_body(reverse, g, o),
        out_shape=jax.ShapeDtypeStruct((ROWS, SLAB, HEAD_DIM), jnp.bfloat16),
        name="carry_back" if reverse else "carry_in",
    )(got)
    back = lax.all_to_all(out, "dp", 0, 0, tiled=True)
    return back.reshape(states.shape)


def head_sum(part):
    for bit in (1, 2, 4):
        part = part + lax.ppermute(part, "head", [(i, i ^ bit) for i in range(8)])
    return part


def edge_factors(rate, flag):
    segment = jnp.cumsum(flag.astype(jnp.int32))
    total = jnp.cumsum(rate, axis=1)
    first = jnp.where(segment[None, :] == 0, jnp.exp(-total), 0.0)
    last = jnp.where(segment[None, :] == segment[-1], jnp.exp(total - total[:, -1:]), 0.0)
    whole = jnp.where(segment[-1] == 0, jnp.exp(-total[:, -1]), 0.0)
    return (total, segment, first, last, whole)


def decay_matrix(total_row, segment):
    count = segment.shape[0]
    places = jnp.arange(count)
    inside = (segment[:, None] == segment[None, :]) & (places[:, None] >= places[None, :])
    return jnp.where(
        inside, jnp.exp(jnp.minimum(total_row[None, :] - total_row[:, None], 0.0)), 0.0
    )


def take_block(array, block_id, length, axis_dim):
    return lax.dynamic_slice_in_dim(array, block_id * length, length, axis_dim)


def place_block(array, block, block_id, axis_dim):
    return lax.dynamic_update_slice_in_dim(array, block, block_id * block.shape[axis_dim], axis_dim)


def contract_first(left, right):
    return lax.dot_general(
        left, right, (((0,), (0,)), ((), ())), preferred_element_type=jnp.float32
    )


def contract_last(left, right):
    return lax.dot_general(
        left, right, (((1,), (1,)), ((), ())), preferred_element_type=jnp.float32
    )


def local(
    queries,
    keys,
    values,
    out_grad,
    norm_gain,
    decay_table,
    decay_index,
    rollout_lengths,
    move_partner,
    move_slot,
):
    row_index = lax.axis_index("dp")
    row_tokens = queries.shape[0]
    heads_here = decay_table.shape[0]
    length = BLOCK_LEN
    partner = move_partner[row_index]
    own_slot = move_slot[row_index]
    apart = jnp.bitwise_xor(partner, row_index)
    levels = take_block(decay_index, own_slot, length, 1).astype(jnp.bfloat16)
    levels = jnp.pad(levels, ((0, 16 - levels.shape[0]), (0, queries.shape[1] - length)))
    outgoing = jnp.concatenate(
        [take_block(member, own_slot, length, 0) for member in (queries, keys, values, out_grad)]
        + [levels]
    )
    arrived = swap_with(outgoing, apart)
    guest = [arrived[n * length : (n + 1) * length] for n in range(4)]
    guest.append(arrived[4 * length : 4 * length + heads_here, :length].astype(jnp.int32))
    packed_q = place_block(queries, guest[0], own_slot, 0)
    packed_k = place_block(keys, guest[1], own_slot, 0)
    packed_v = place_block(values, guest[2], own_slot, 0)
    packed_dy = place_block(out_grad, guest[3], own_slot, 0)
    packed_index = place_block(decay_index, guest[4], own_slot, 1)
    level_ids = jnp.arange(decay_table.shape[1], dtype=jnp.int32)
    rate = jnp.sum(
        jnp.where(packed_index[:, :, None] == level_ids, decay_table[:, None, :], 0.0), axis=2
    )
    starts = jnp.cumsum(rollout_lengths) - rollout_lengths
    position = row_index * row_tokens + jnp.arange(row_tokens, dtype=jnp.int32)
    flag = jnp.any(position[:, None] == starts[None, :], axis=1)
    total, segment, first, last, whole = edge_factors(rate, flag)
    head_cols = []
    local_states = []
    for head_pos in range(heads_here):
        columns = slice(head_pos * HEAD_DIM, (head_pos + 1) * HEAD_DIM)
        head_cols.append(columns)
        gated_values = (packed_v[:, columns].astype(jnp.float32) * last[head_pos][:, None]).astype(
            jnp.bfloat16
        )
        local_states.append(contract_first(packed_k[:, columns], gated_values))
    stacked = jnp.stack(local_states)
    carry_half = entering(stacked, whole, False)
    decays = []
    weight_list = []
    retained_parts = []
    for head_pos in range(heads_here):
        columns = head_cols[head_pos]
        query_head = packed_q[:, columns]
        decay = decay_matrix(total[head_pos], segment)
        scores = contract_last(query_head, packed_k[:, columns])
        weights = (scores * decay / HEAD_DIM).astype(jnp.bfloat16)
        inner_part = jnp.dot(weights, packed_v[:, columns], preferred_element_type=jnp.float32)
        cross_part = (
            first[head_pos][:, None]
            * jnp.dot(query_head, carry_half[head_pos], preferred_element_type=jnp.float32)
            / HEAD_DIM
        )
        decays.append(decay)
        weight_list.append(weights)
        retained_parts.append(inner_part + cross_part)
    retained = jnp.concatenate(retained_parts, axis=1)
    scaled = norm_gain * packed_dy.astype(jnp.float32)
    squares, inner = head_sum(
        jnp.stack([jnp.sum(retained * retained, axis=1), jnp.sum(scaled * retained, axis=1)])
    )
    recip = lax.rsqrt(squares / FEATURES + EPSILON)
    norm_grad = (
        recip[:, None] * scaled - (recip**3 * inner / FEATURES)[:, None] * retained
    ).astype(jnp.bfloat16)
    back_locals = []
    for head_pos in range(heads_here):
        columns = head_cols[head_pos]
        weighted = (norm_grad[:, columns].astype(jnp.float32) * first[head_pos][:, None]).astype(
            jnp.bfloat16
        )
        back_locals.append(contract_first(packed_q[:, columns], weighted) / HEAD_DIM)
    back_stack = jnp.stack(back_locals)
    back_half = entering(back_stack, whole, True)
    query_parts = []
    key_parts = []
    value_parts = []
    for head_pos in range(heads_here):
        columns = head_cols[head_pos]
        query_head = packed_q[:, columns]
        key_head = packed_k[:, columns]
        value_head = packed_v[:, columns]
        grad_head = norm_grad[:, columns]
        grad_scores = contract_last(grad_head, value_head)
        grad_weights = (grad_scores * decays[head_pos] / HEAD_DIM).astype(jnp.bfloat16)
        query_part = jnp.dot(grad_weights, key_head, preferred_element_type=jnp.float32)
        query_part = (
            query_part
            + first[head_pos][:, None] * contract_last(grad_head, carry_half[head_pos]) / HEAD_DIM
        )
        key_part = contract_first(grad_weights, query_head)
        key_part = key_part + last[head_pos][:, None] * contract_last(
            value_head, back_half[head_pos]
        )
        value_part = contract_first(weight_list[head_pos], grad_head)
        value_part = value_part + last[head_pos][:, None] * jnp.dot(
            key_head, back_half[head_pos], preferred_element_type=jnp.float32
        )
        query_parts.append(query_part)
        key_parts.append(key_part)
        value_parts.append(value_part)
    packed_grads = (
        jnp.concatenate(query_parts, axis=1).astype(jnp.bfloat16),
        jnp.concatenate(key_parts, axis=1).astype(jnp.bfloat16),
        jnp.concatenate(value_parts, axis=1).astype(jnp.bfloat16),
    )
    leaving = jnp.concatenate([take_block(member, own_slot, length, 0) for member in packed_grads])
    came = swap_with(leaving, apart)
    returned = [came[n * length : (n + 1) * length] for n in range(3)]
    query_grad = place_block(packed_grads[0], returned[0], own_slot, 0)
    key_grad = place_block(packed_grads[1], returned[1], own_slot, 0)
    value_grad = place_block(packed_grads[2], returned[2], own_slot, 0)
    return (query_grad, key_grad, value_grad)


def solution(mesh):
    placed = (
        P("dp", "head"),
        P("dp", "head"),
        P("dp", "head"),
        P("dp", "head"),
        P("head"),
        P("head", None),
        P("head", "dp"),
        P(),
        P(),
        P(),
    )
    return jax.shard_map(
        local,
        mesh=mesh,
        in_specs=placed,
        out_specs=(P("dp", "head"), P("dp", "head"), P("dp", "head")),
        check_vma=False,
    )
```
